32 devices in a mesh: ctx: 8 (over z, y), head: 4 (over x, core).
Axes of the slice: x: 2, y: 2, z: 4, core: 2. Of those that a mesh axis runs over, the one named last changes fastest.
Arguments:
- query_rows: bfloat16 [8192, 4096], P('ctx', 'head'), may hold values from -6 to 6
- key_rows: bfloat16 [8192, 4096], P('ctx', 'head'), may hold values from -6 to 6
- value_rows: bfloat16 [8192, 4096], P('ctx', 'head'), may hold values from -6 to 6
- level_gate: float32 [6, 32, 8192], P(None, 'head', 'ctx'), may hold values from 0 to 2.5, as said below
- out_weight: bfloat16 [4096, 4096], P('head'), may hold values from -0.09375 to 0.09375
Outputs:
- output: bfloat16 [8192, 4096], P(('ctx', 'head'))
The draws below stay inside these ranges and needn't reach their ends.
Inputs may be any that keep to these rules, and one draw needn't show every extreme that they name: `level_gate`: every gate weight is positive.
All inputs are finite; a program needn't handle non-finite values.
Results may differ from the reference program's by a relative error of at most 0.015.
Values may be sent and summed in bfloat16 or wider, within the bound.
A program may use at most 128 MiB of HBM per device.

```python
import math
import jax
import jax.numpy as jnp
from jax import lax

H = 32
DH = 128
D = 4096
C = 256
LEVELS = 6
SEQ = 8192
N_HEAD = 4


def draw_level_gate(key, part):
    level_ids = jnp.arange(LEVELS, dtype=jnp.float32)[:, None, None]
    base_gate = jnp.exp(jax.random.uniform(key, (LEVELS, H, SEQ), jnp.float32, math.log(0.25), math.log(2.5)))
    return base_gate * jnp.exp(-0.5 * math.log(2.0) * level_ids)


def levels(own_key, dims, pieces, least, high):
    loudness, own = 1.0, jax.random.fold_in(own_key, 6)
    for position, shards_of in pieces:
        steps = jnp.exp(jax.random.uniform(jax.random.fold_in(own, position), (shards_of,), jnp.float32, least / len(pieces), high / len(pieces)))
        loudness = loudness * jnp.repeat(steps, dims[position] // shards_of).reshape([-1 if axis == position else 1 for axis in range(len(dims))])
    return loudness


def scatter_about(key, extent, width, limit, pieces=(), kind=jnp.bfloat16):
    entries = width * jax.random.normal(key, extent, jnp.float32)
    if pieces:
        entries = entries * levels(key, extent, pieces, -0.22, 0.18)
    return jnp.clip(entries, -limit, limit).astype(kind)


def setup_inputs(seed: int = 0) -> dict:
    seeds = jax.random.split(jax.random.key(seed), 6)
    query_rows = scatter_about(seeds[0], (SEQ, H * DH), 1.0, 6.0, ((0, 8), (1, 4)))
    key_rows = scatter_about(seeds[1], (SEQ, H * DH), 1.0, 6.0, ((0, 8), (1, 4)))
    value_rows = scatter_about(seeds[2], (SEQ, H * DH), 1.0, 6.0, ((0, 8), (1, 4)))
    level_gate = draw_level_gate(jax.random.fold_in(seeds[5], 71), 0)
    out_weight = scatter_about(seeds[4], (H * DH, D), (H * DH) ** -0.5, 0.09375, ((0, 4),))
    return {"query_rows": query_rows, "key_rows": key_rows, "value_rows": value_rows, "level_gate": level_gate, "out_weight": out_weight}


EPS = 1e-06

def head_block(query_rows, key_rows, value_rows, level_gate, head_id):
    seq_len = query_rows.shape[0]
    num_stretches = seq_len // C
    col_start = (head_id * DH).astype(jnp.int32)
    query_stretches = lax.dynamic_slice_in_dim(query_rows, col_start, DH, 1).reshape(num_stretches, C, DH).astype(jnp.float32)
    key_stretches = lax.dynamic_slice_in_dim(key_rows, col_start, DH, 1).reshape(num_stretches, C, DH).astype(jnp.float32)
    value_stretches = lax.dynamic_slice_in_dim(value_rows, col_start, DH, 1).reshape(num_stretches, C, DH).astype(jnp.float32)
    gates = lax.dynamic_slice_in_dim(level_gate, head_id.astype(jnp.int32), 1, 1)[:, 0, :].reshape(LEVELS, num_stretches, C)
    scores = jnp.einsum('cti,csi->cts', query_stretches, key_stretches)
    row_ids = lax.broadcasted_iota(jnp.int32, (C, C), 0)
    col_ids = lax.broadcasted_iota(jnp.int32, (C, C), 1)
    weights = (jnp.where(row_ids >= col_ids, scores, 0.0) * gates[0][:, :, None]).astype(jnp.bfloat16)
    combined = jnp.einsum('cts,csj->ctj', weights.astype(jnp.float32), value_stretches)
    stretch_state = jnp.einsum('csi,csj->cij', key_stretches, value_stretches)
    stretch_ids = jnp.arange(num_stretches, dtype=jnp.int32)
    for level_bit in range(LEVELS - 1):
        span_size = 2 ** level_bit
        grouped = stretch_state.reshape(num_stretches // span_size, span_size, DH, DH).sum(axis=1)
        owner_block = stretch_ids // span_size
        bucket = grouped[jnp.maximum(owner_block - 1, 0)].astype(jnp.bfloat16)
        readout = jnp.einsum('cti,cij->ctj', query_stretches, bucket.astype(jnp.float32))
        combined = combined + jnp.where((owner_block % 2 == 1)[:, None, None], readout * gates[level_bit + 1][:, :, None], 0.0)
    normed = combined * lax.rsqrt(lax.optimization_barrier(jnp.mean(combined * combined, axis=-1, keepdims=True)) + EPS)
    return normed.astype(jnp.bfloat16).reshape(seq_len, DH)

def reference(query_rows, key_rows, value_rows, level_gate, out_weight):
    head_ids = jnp.arange(H, dtype=jnp.int32)
    blocks = lax.map(lambda head_id: head_block(query_rows, key_rows, value_rows, level_gate, head_id), head_ids)
    seq_len = query_rows.shape[0]
    normed = jnp.transpose(blocks, (1, 0, 2)).reshape(seq_len, H * DH)
    group_cols = H // N_HEAD * DH
    result = jnp.zeros((seq_len, D), jnp.float32)
    for group_index in range(N_HEAD):
        lower = group_index * group_cols
        upper = lower + group_cols
        partial_value = jnp.dot(normed[:, lower:upper], out_weight[lower:upper], preferred_element_type=jnp.float32)
        partial_value = lax.optimization_barrier(partial_value.astype(jnp.bfloat16)).astype(jnp.float32)
        result = result + partial_value
    return result.astype(jnp.bfloat16)
```

```python
import functools

import jax
import jax.numpy as jnp
from jax import lax
from jax.experimental import pallas as pl
from jax.experimental.pallas import tpu as pltpu
from jax.sharding import PartitionSpec as P

C = 256
EPS = 1e-06
CHUNKS = 8
TILE = 512
MESH = pl.DeviceIdType.MESH
F32 = jnp.float32
BF16 = jnp.bfloat16


def buckets_of(stretches):
    keys = []
    span = 1
    while span < stretches:
        keys += [(span, block) for block in range(0, stretches // span, 2)]
        span *= 2
    return keys


def kernel(
    ctx_size, heads, levels,
    q_hbm, k_hbm, v_hbm, g_hbm, w_hbm, out,
    q, k, v, g, gate_cols, w, comb, run, near, s_buf, r_buf,
    to_sib, from_sib, mine, p_send, p_recv, own,
    load_sem, st_send, st_recv, hand_send, w_send, w_recv, n_send, n_recv, p_ssem, p_rsem,
):
    ctx_bits = ctx_size.bit_length() - 1
    tokens, width = q.shape[0], q.shape[1] // heads
    stretches = tokens // C
    bits = stretches.bit_length() - 1
    per = heads // CHUNKS
    half_chunks = CHUNKS // 2
    rows = own.shape[0]
    tiles = p_send.shape[0]
    keys = buckets_of(stretches)
    me = lax.axis_index("ctx")
    head_at = lax.axis_index("head")
    digits = [lax.rem(lax.div(me, 2**b), 2) for b in range(ctx_bits)]
    ahead = me + 2
    has_next = (ahead < ctx_size).astype(jnp.int32)
    has_prev = (me >= 2).astype(jnp.int32)
    wanted = [lax.rem(lax.div(ahead, 2**b), 2) * has_next for b in range(ctx_bits)]
    partner = {"ctx": me + 1 - 2 * digits[0]}
    nxt, prev = {"ctx": ahead}, {"ctx": me - 2}
    core = lax.rem(head_at, 2)
    pair = lax.div(head_at, 2)
    other = 1 - pair
    sib = {"head": pair * 2 + 1 - core}
    far_dev = {"head": other * 2 + core}

    cols = q.shape[1]
    part_cols = cols // 2

    def half_copy(src, dst, which, sem):
        at = pl.ds(pl.multiple_of(which * part_cols, part_cols), part_cols)
        return pltpu.make_async_copy(src.at[:, at], dst.at[:, at], load_sem.at[sem])

    first = 1 - digits[0]
    kv_loads = [
        [half_copy(k_hbm, k, first, 0), half_copy(v_hbm, v, first, 1)],
        [half_copy(k_hbm, k, digits[0], 2), half_copy(v_hbm, v, digits[0], 3)],
    ]
    q_load = pltpu.make_async_copy(q_hbm, q, load_sem.at[4])
    g_load = pltpu.make_async_copy(g_hbm, g, load_sem.at[5])
    w_load = pltpu.make_async_copy(w_hbm, w.at[0], load_sem.at[6])
    for copy in kv_loads[0] + kv_loads[1] + [q_load, g_load]:
        copy.start()

    barrier = pltpu.get_barrier_semaphore()
    for device in (partner, sib, far_dev):
        pl.semaphore_signal(barrier, inc=1, device_id=device, device_id_type=MESH)

    @pl.when(has_next == 1)
    def _():
        pl.semaphore_signal(barrier, inc=1, device_id=nxt, device_id_type=MESH)

    @pl.when(has_prev == 1)
    def _():
        pl.semaphore_signal(barrier, inc=1, device_id=prev, device_id_type=MESH)

    def w_copy(tile):
        at = pl.ds(pl.multiple_of(tile * TILE, TILE), TILE)
        return pltpu.make_async_remote_copy(
            src_ref=w_hbm.at[:, at], dst_ref=w.at[1, :, at],
            send_sem=w_send.at[tile], recv_sem=w_recv.at[tile],
            device_id=sib, device_id_type=MESH,
        )

    def state_copy(level, chunk, relay=False):
        part = pl.ds(chunk * per, per)
        return pltpu.make_async_remote_copy(
            src_ref=(r_buf if relay else s_buf).at[level, part], dst_ref=r_buf.at[level, part],
            send_sem=st_send.at[level, chunk], recv_sem=st_recv.at[level, chunk],
            device_id=nxt if level else partner, device_id_type=MESH,
        )

    def hand_copy(level, chunk):
        part = pl.ds(chunk * per, per)
        return pltpu.make_async_remote_copy(
            src_ref=r_buf.at[level, part], dst_ref=r_buf.at[level, part],
            send_sem=hand_send.at[level, chunk], recv_sem=st_recv.at[level, chunk],
            device_id=partner, device_id_type=MESH,
        )

    def ours(n):
        return lax.rem(n + digits[0] * half_chunks, CHUNKS)

    def theirs(n):
        return lax.rem(n + (1 - digits[0]) * half_chunks, CHUNKS)

    def pass_on(level, chunk):
        if level < ctx_bits:
            @pl.when((digits[level] == 0) & (wanted[level] == 1))
            def _():
                part = pl.ds(chunk * per, per)
                s_buf[level, part] = run[part].astype(BF16)
                state_copy(level, chunk).start()

    def service(level, n):
        chunk = ours(n)
        part = pl.ds(chunk * per, per)
        if level == 0:
            state_copy(0, chunk).wait_recv()
            if ctx_bits > 1:
                run[part] = run[part] + r_buf[0, part].astype(F32)
                pass_on(1, chunk)
            return

        @pl.when(digits[level] == 1)
        def _():
            state_copy(level, chunk).wait_recv()
            if level > 1:
                @pl.when(wanted[level] == 1)
                def _():
                    state_copy(level, chunk, relay=True).start()

                hand_copy(level, chunk).start()
            if level + 1 < ctx_bits:
                @pl.when(n < half_chunks)
                def _():
                    run[part] = run[part] + r_buf[level, part].astype(F32)
                    pass_on(level + 1, chunk)

    def lanes(head):
        return pl.ds(pl.multiple_of(head * width, width), width)

    def states(chunk):
        for inner in range(per):
            head = chunk * per + inner
            col = lanes(head)
            sums = {}
            for c in range(stretches):
                token = pl.ds(c * C, C)
                sums[1, c] = lax.dot_general(
                    k[token, col], v[token, col], (((0,), (0,)), ((), ())),
                    preferred_element_type=F32,
                )
            span = 1
            while span < stretches:
                for block in range(stretches // span // 2):
                    sums[span * 2, block] = sums[span, block * 2] + sums[span, block * 2 + 1]
                span *= 2
            for n, key in enumerate(keys):
                near[head, n] = sums[key].astype(BF16)
            run[head] = sums[stretches, 0]
            s_buf[0, head] = sums[stretches, 0].astype(BF16)

    for copy in kv_loads[0]:
        copy.wait()

    @pl.loop(0, half_chunks)
    def _(n):
        states(theirs(n))

    pl.semaphore_wait(barrier, 3 + has_next + has_prev)

    @pl.loop(0, half_chunks)
    def _(n):
        state_copy(0, theirs(n)).start()

    for copy in kv_loads[1]:
        copy.wait()

    @pl.loop(half_chunks, CHUNKS)
    def _(n):
        states(theirs(n))
        state_copy(0, theirs(n)).start()

    @pl.loop(0, tiles)
    def _(tile):
        w_copy(tile).start()

    w_load.start()
    for level in range(1, ctx_bits):
        @pl.when(digits[level] == 0)
        def _():
            r_buf[level] = jnp.zeros(r_buf.shape[1:], BF16)

    q_load.wait()
    g_load.wait()
    pad = gate_cols.shape[2] - levels
    for head in range(heads):
        strips = [g[level, head : head + 1, :] for level in range(levels)]
        if pad:
            strips.append(jnp.zeros((pad, tokens), F32))
        gate_cols[head] = jnp.concatenate(strips, axis=0).T

    keep = lax.broadcasted_iota(jnp.int32, (C, C), 0) >= lax.broadcasted_iota(
        jnp.int32, (C, C), 1
    )

    def attend(duo, odd, head):
        block = duo * 2 + odd
        token = pl.ds(pl.multiple_of(block * C, C), C)
        col = lanes(head)
        gates = gate_cols[head, token, :]
        query = q[token, col]
        scores = lax.dot_general(
            query, k[token, col], (((1,), (1,)), ((), ())), preferred_element_type=F32
        )
        weights = (jnp.where(keep, scores, 0.0) * gates[:, 0:1]).astype(BF16)
        total = jnp.dot(weights, v[token, col], preferred_element_type=F32)
        if odd:
            read = jnp.dot(query, near[head, duo], preferred_element_type=F32)
            total = total + read * gates[:, 1:2]
        at = stretches // 2
        for b in range(1, bits):
            span = lax.div(duo, 2 ** (b - 1))
            use = lax.rem(span, 2).astype(F32)
            read = jnp.dot(
                query, near[head, at + lax.div(span, 2)], preferred_element_type=F32
            )
            total = total + read * (gates[:, b + 1 : b + 2] * use)
            at += stretches // 2 ** (b + 1)
        return total

    def attend_pair(duo, chunk):
        for inner in range(per):
            head = chunk * per + inner
            for odd in range(2):
                token = pl.ds(pl.multiple_of((duo * 2 + odd) * C, C), C)
                comb[token, lanes(head)] = attend(duo, odd, head)

    lags = [1 + 3 * level for level in range(ctx_bits)]
    counts = [CHUNKS if level < 2 else half_chunks for level in range(ctx_bits)]
    steps = max([CHUNKS] + [lag + count for lag, count in zip(lags, counts)])

    @pl.loop(0, steps)
    def _(n):
        for level in range(ctx_bits):
            @pl.when((n >= lags[level]) & (n < lags[level] + counts[level]))
            def _():
                service(level, n - lags[level])

        @pl.when(n < CHUNKS)
        def _():
            attend_pair(other, n)

    scale = [digit.astype(F32) for digit in digits]

    def sib_copy(n, chunk):
        at = pl.ds(pl.multiple_of(chunk * per * width, per * width), per * width)
        return pltpu.make_async_remote_copy(
            src_ref=to_sib.at[n, :, at], dst_ref=from_sib.at[n, :, at],
            send_sem=n_send.at[n, chunk], recv_sem=n_recv.at[n, chunk],
            device_id=sib, device_id_type=MESH,
        )

    def finish(block, chunk, dst):
        token = pl.ds(pl.multiple_of(block * rows, rows), rows)
        for inner in range(per):
            head = chunk * per + inner
            col = lanes(head)
            gates = gate_cols[head, token, :]
            query = q[token, col]
            total = comb[token, col]
            for level in range(ctx_bits):
                read = jnp.dot(query, r_buf[level, head], preferred_element_type=F32)
                at = bits + 1 + level
                total = total + read * (gates[:, at : at + 1] * scale[level])
            mean = jnp.mean(total * total, axis=-1, keepdims=True)
            dst[:, col] = (total * lax.rsqrt(mean + EPS)).astype(BF16)

    def p_copy(tile):
        return pltpu.make_async_remote_copy(
            src_ref=p_send.at[tile], dst_ref=p_recv.at[tile],
            send_sem=p_ssem.at[tile], recv_sem=p_rsem.at[tile],
            device_id=far_dev, device_id_type=MESH,
        )

    def project(n, part, tile):
        at = pl.ds(pl.multiple_of(tile * TILE, TILE), TILE)
        return jnp.dot((from_sib if part else mine)[n], w[part, :, at], preferred_element_type=F32)

    def handed(n):
        for level in range(2, ctx_bits):
            @pl.when(digits[level] == 1)
            def _():
                hand_copy(level, theirs(n)).wait_recv()

    def finish_chunk(n, duo, chunk):
        finish(duo * 2 + 1 - core, chunk, to_sib.at[n])
        sib_copy(n, chunk).start()
        finish(duo * 2 + core, chunk, mine.at[n])

    @pl.loop(0, half_chunks)
    def _(n):
        finish_chunk(0, other, ours(n))

    @pl.loop(0, half_chunks)
    def _(n):
        handed(n)
        finish_chunk(0, other, theirs(n))

    w_load.wait()

    @pl.loop(0, tiles)
    def _(tile):
        near_part = project(0, 0, tile)

        @pl.when(tile == 0)
        def _():
            for chunk in range(CHUNKS):
                sib_copy(0, chunk).wait_recv()

        w_copy(tile).wait_recv()
        p_send[tile] = (near_part + project(0, 1, tile)).astype(BF16)
        p_copy(tile).start()

    @pl.loop(0, CHUNKS)
    def _(chunk):
        attend_pair(pair, chunk)

    @pl.loop(0, CHUNKS)
    def _(chunk):
        finish_chunk(1, pair, chunk)

    for chunk in range(CHUNKS):
        sib_copy(1, chunk).wait_recv()

    @pl.loop(0, tiles)
    def _(tile):
        own[:, pl.ds(pl.multiple_of(tile * TILE, TILE), TILE)] = project(1, 0, tile) + project(1, 1, tile)

    @pl.loop(0, tiles)
    def _(tile):
        p_copy(tile).wait_send()
        w_copy(tile).wait_send()

    for n in range(2):
        for chunk in range(CHUNKS):
            sib_copy(n, chunk).wait_send()

    @pl.loop(0, CHUNKS)
    def _(chunk):
        state_copy(0, chunk).wait_send()

    for level in range(1, ctx_bits):
        @pl.when(wanted[level] == 1)
        def _():
            @pl.loop(0, counts[level])
            def _(n):
                state_copy(level, ours(n)).wait_send()

        if level > 1:
            @pl.when(digits[level] == 1)
            def _():
                @pl.loop(0, half_chunks)
                def _(n):
                    hand_copy(level, ours(n)).wait_send()

    @pl.loop(0, tiles)
    def _(tile):
        at = pl.ds(pl.multiple_of(tile * TILE, TILE), TILE)
        p_copy(tile).wait_recv()
        out[:, at] = (own[:, at] + p_recv[tile].astype(F32)).astype(BF16)


def on_device(query_rows, key_rows, value_rows, level_gate, out_weight):
    tokens, cols = query_rows.shape
    levels, heads, _ = level_gate.shape
    width = cols // heads
    model = out_weight.shape[1]
    rows = tokens // lax.axis_size("head")
    ctx_size = lax.axis_size("ctx")
    ctx_bits = ctx_size.bit_length() - 1
    tiles = model // TILE
    near = len(buckets_of(tokens // C))
    dma = pltpu.SemaphoreType.DMA
    flops = 2 * tokens * cols * (model + 2 * C + width * 7)
    operands = [
        pltpu.with_memory_space_constraint(x, pltpu.HBM)
        for x in (query_rows, key_rows, value_rows, level_gate, out_weight)
    ]
    return pl.pallas_call(
        functools.partial(kernel, ctx_size, heads, levels),
        out_shape=pltpu.VMEM((rows, model), BF16),
        in_specs=[pl.BlockSpec(memory_space=pl.ANY)] * 5,
        out_specs=pl.BlockSpec(memory_space=pltpu.VMEM),
        scratch_shapes=[
            pltpu.VMEM((tokens, cols), BF16),
            pltpu.VMEM((tokens, cols), BF16),
            pltpu.VMEM((tokens, cols), BF16),
            pltpu.VMEM((levels, heads, tokens), F32),
            pltpu.VMEM((heads, tokens, -(-levels // 8) * 8), F32),
            pltpu.VMEM((2, cols, model), BF16),
            pltpu.VMEM((tokens, cols), F32),
            pltpu.VMEM((heads, width, width), F32),
            pltpu.VMEM((heads, near, width, width), BF16),
            pltpu.VMEM((ctx_bits, heads, width, width), BF16),
            pltpu.VMEM((ctx_bits, heads, width, width), BF16),
            pltpu.VMEM((2, rows, cols), BF16),
            pltpu.VMEM((2, rows, cols), BF16),
            pltpu.VMEM((2, rows, cols), BF16),
            pltpu.VMEM((tiles, rows, TILE), BF16),
            pltpu.VMEM((tiles, rows, TILE), BF16),
            pltpu.VMEM((rows, model), F32),
            dma((7,)),
            dma((ctx_bits, CHUNKS)),
            dma((ctx_bits, CHUNKS)),
            dma((ctx_bits, CHUNKS)),
            dma((tiles,)),
            dma((tiles,)),
            dma((2, CHUNKS)),
            dma((2, CHUNKS)),
            dma((tiles,)),
            dma((tiles,)),
        ],
        compiler_params=pltpu.CompilerParams(
            collective_id=0, has_side_effects=True, vmem_limit_bytes=52 * 1024 * 1024
        ),
        cost_estimate=pl.CostEstimate(
            flops=flops, bytes_accessed=20 * 1024 * 1024, transcendentals=tokens * heads
        ),
        name="levels_project",
    )(*operands)


def solution(mesh):
    in_specs = (
        P("ctx", "head"),
        P("ctx", "head"),
        P("ctx", "head"),
        P(None, "head", "ctx"),
        P("head", None),
    )
    out_specs = P(("ctx", "head"), None)
    return jax.shard_map(
        on_device, mesh=mesh, in_specs=in_specs, out_specs=out_specs, check_vma=False
    )
```

```python
import functools

import jax
import jax.numpy as jnp
from jax import lax
from jax.experimental import pallas as pl
from jax.experimental.pallas import tpu as pltpu
from jax.sharding import PartitionSpec as P

C = 256
EPS = 1e-06
CHUNKS = 4
TILE = 256
MESH = pl.DeviceIdType.MESH
F32 = jnp.float32
BF16 = jnp.bfloat16


def buckets_of(stretches):
    keys = []
    span = 1
    while span < stretches:
        keys += [(span, block) for block in range(0, stretches // span, 2)]
        span *= 2
    return keys


def kernel(
    ctx_size, heads, levels,
    q_hbm, k_hbm, v_hbm, g_hbm, w_hbm, out,
    q, k, v, g, gate_cols, w, comb, run, near, s_buf, r_buf, gated,
    to_sib, from_sib, mine, p_send, p_recv, own,
    load_sem, st_send, st_recv, hand_send, over_send, w_send, w_recv, n_send, n_recv, p_ssem, p_rsem,
):
    ctx_bits = ctx_size.bit_length() - 1
    tokens, width = q.shape[0], q.shape[1] // heads
    stretches = tokens // C
    bits = stretches.bit_length() - 1
    per = heads // CHUNKS
    half = CHUNKS // 2
    rows = own.shape[0]
    tiles = p_send.shape[0]
    keys = buckets_of(stretches)
    me = lax.axis_index("ctx")
    head_at = lax.axis_index("head")
    digits = [lax.rem(lax.div(me, 2**b), 2) for b in range(ctx_bits)]
    ahead = me + 2
    has_next = (ahead < ctx_size).astype(jnp.int32)
    has_prev = (me >= 2).astype(jnp.int32)
    wanted = [lax.rem(lax.div(ahead, 2**b), 2) * has_next for b in range(ctx_bits)]
    skips = digits[1] * (1 - digits[2]) if ctx_bits > 2 else jnp.int32(0)
    skipped = digits[1] * digits[2] if ctx_bits > 2 else jnp.int32(0)
    over, under = {"ctx": me + 4}, {"ctx": me - 4}
    partner = {"ctx": me + 1 - 2 * digits[0]}
    nxt, prev = {"ctx": ahead}, {"ctx": me - 2}
    core = lax.rem(head_at, 2)
    pair = lax.div(head_at, 2)
    other = 1 - pair
    sib = {"head": pair * 2 + 1 - core}
    far_dev = {"head": other * 2 + core}

    barrier = pltpu.get_barrier_semaphore()
    for device in (partner, sib, far_dev):
        pl.semaphore_signal(barrier, inc=1, device_id=device, device_id_type=MESH)

    @pl.when(has_next == 1)
    def _():
        pl.semaphore_signal(barrier, inc=1, device_id=nxt, device_id_type=MESH)

    @pl.when(has_prev == 1)
    def _():
        pl.semaphore_signal(barrier, inc=1, device_id=prev, device_id_type=MESH)

    @pl.when(skips == 1)
    def _():
        pl.semaphore_signal(barrier, inc=1, device_id=over, device_id_type=MESH)

    @pl.when(skipped == 1)
    def _():
        pl.semaphore_signal(barrier, inc=1, device_id=under, device_id_type=MESH)

    cols = q.shape[1]
    part_cols = cols // 2

    def half_copy(src, dst, which, sem):
        at = pl.ds(pl.multiple_of(which * part_cols, part_cols), part_cols)
        return pltpu.make_async_copy(src.at[:, at], dst.at[:, at], load_sem.at[sem])

    first = 1 - digits[0]
    kv_loads = [
        [half_copy(k_hbm, k, first, 0), half_copy(v_hbm, v, first, 1)],
        [half_copy(k_hbm, k, digits[0], 2), half_copy(v_hbm, v, digits[0], 3)],
    ]
    q_load = pltpu.make_async_copy(q_hbm, q, load_sem.at[4])
    g_load = pltpu.make_async_copy(g_hbm, g, load_sem.at[5])
    w_load = pltpu.make_async_copy(w_hbm, w.at[0], load_sem.at[6])
    for copy in kv_loads[0] + kv_loads[1] + [q_load, g_load]:
        copy.start()

    def w_copy(tile):
        at = pl.ds(pl.multiple_of(tile * TILE, TILE), TILE)
        return pltpu.make_async_remote_copy(
            src_ref=w_hbm.at[:, at], dst_ref=w.at[1, :, at],
            send_sem=w_send.at[tile], recv_sem=w_recv.at[tile],
            device_id=sib, device_id_type=MESH,
        )

    def slot(level):
        return pl.ds(level * width, width)

    def group(chunk):
        return pl.ds(chunk * per, per)

    def state_copy(level, chunk, relay=False):
        came = r_buf.at[group(chunk), slot(level)]
        return pltpu.make_async_remote_copy(
            src_ref=came if relay else s_buf.at[level, group(chunk)], dst_ref=came,
            send_sem=st_send.at[level, chunk], recv_sem=st_recv.at[level, chunk],
            device_id=nxt if level else partner, device_id_type=MESH,
        )

    direct = half // 2

    def over_copy(chunk):
        return pltpu.make_async_remote_copy(
            src_ref=s_buf.at[2, group(chunk)], dst_ref=r_buf.at[group(chunk), slot(2)],
            send_sem=over_send.at[chunk], recv_sem=st_recv.at[2, chunk],
            device_id=over, device_id_type=MESH,
        )

    def flip(n):
        return n + skipped * (half - 1 - 2 * n)

    def hand_copy(level, chunk):
        came = r_buf.at[group(chunk), slot(level)]
        return pltpu.make_async_remote_copy(
            src_ref=came, dst_ref=came,
            send_sem=hand_send.at[level, chunk], recv_sem=st_recv.at[level, chunk],
            device_id=partner, device_id_type=MESH,
        )

    def ours(n):
        return lax.rem(n + digits[0] * half, CHUNKS)

    def theirs(n):
        return lax.rem(n + (1 - digits[0]) * half, CHUNKS)

    def pass_on(level, chunk, n):
        if level < ctx_bits:
            @pl.when((digits[level] == 0) & (wanted[level] == 1))
            def _():
                s_buf[level, group(chunk)] = run[group(chunk)].astype(BF16)
                state_copy(level, chunk).start()
                if level == 2:
                    @pl.when(n >= direct)
                    def _():
                        over_copy(chunk).start()

    def service(level, n):
        if level == 2:
            n = flip(n)
        chunk = ours(n)
        if level == 0:
            state_copy(0, chunk).wait_recv()
            if ctx_bits > 1:
                run[group(chunk)] = run[group(chunk)] + r_buf[group(chunk), slot(0)].astype(F32)
                pass_on(1, chunk, n)
            return

        @pl.when(digits[level] == 1)
        def _():
            state_copy(level, chunk).wait_recv()
            if level > 1:
                @pl.when((wanted[level] == 1) & ((n < direct) if level == 2 else True))
                def _():
                    state_copy(level, chunk, relay=True).start()

                hand_copy(level, chunk).start()
            if level + 1 < ctx_bits:
                @pl.when(n < half)
                def _():
                    run[group(chunk)] = run[group(chunk)] + r_buf[group(chunk), slot(level)].astype(F32)
                    pass_on(level + 1, chunk, n)

    def lanes(head):
        return pl.ds(pl.multiple_of(head * width, width), width)

    def states(chunk):
        for inner in range(per):
            head = chunk * per + inner
            col = lanes(head)
            sums = {}
            for c in range(stretches):
                token = pl.ds(c * C, C)
                sums[1, c] = lax.dot_general(
                    k[token, col], v[token, col], (((0,), (0,)), ((), ())),
                    preferred_element_type=F32,
                )
            span = 1
            while span < stretches:
                for block in range(stretches // span // 2):
                    sums[span * 2, block] = sums[span, block * 2] + sums[span, block * 2 + 1]
                span *= 2
            for n, key in enumerate(keys):
                near[head, n] = sums[key].astype(BF16)
            run[head] = sums[stretches, 0]
            s_buf[0, head] = sums[stretches, 0].astype(BF16)

    for copy in kv_loads[0]:
        copy.wait()

    @pl.loop(0, half)
    def _(n):
        states(theirs(n))

    pl.semaphore_wait(barrier, 3 + has_next + has_prev + skips + skipped)

    @pl.loop(0, half)
    def _(n):
        state_copy(0, theirs(n)).start()

    for copy in kv_loads[1]:
        copy.wait()

    @pl.loop(half, CHUNKS)
    def _(n):
        states(theirs(n))
        state_copy(0, theirs(n)).start()

    @pl.loop(0, tiles)
    def _(tile):
        w_copy(tile).start()

    w_load.start()
    for level in range(1, ctx_bits):
        @pl.when(digits[level] == 0)
        def _():
            for head in range(heads):
                r_buf[head, slot(level)] = jnp.zeros((width, width), BF16)

    q_load.wait()
    g_load.wait()
    pad = gate_cols.shape[2] - levels
    for head in range(heads):
        strips = [g[level, head : head + 1, :] for level in range(levels)]
        if pad:
            strips.append(jnp.zeros((pad, tokens), F32))
        gate_cols[head] = jnp.concatenate(strips, axis=0).T

    keep = lax.broadcasted_iota(jnp.int32, (C, C), 0) >= lax.broadcasted_iota(
        jnp.int32, (C, C), 1
    )

    def attend(duo, odd, head):
        block = duo * 2 + odd
        token = pl.ds(pl.multiple_of(block * C, C), C)
        col = lanes(head)
        gates = gate_cols[head, token, :]
        query = q[token, col]
        scores = lax.dot_general(
            query, k[token, col], (((1,), (1,)), ((), ())), preferred_element_type=F32
        )
        weights = (jnp.where(keep, scores, 0.0) * gates[:, 0:1]).astype(BF16)
        total = jnp.dot(weights, v[token, col], preferred_element_type=F32)
        if odd:
            read = jnp.dot(query, near[head, duo], preferred_element_type=F32)
            total = total + read * gates[:, 1:2]
        at = stretches // 2
        for b in range(1, bits):
            span = lax.div(duo, 2 ** (b - 1))
            use = lax.rem(span, 2).astype(F32)
            read = jnp.dot(
                query, near[head, at + lax.div(span, 2)], preferred_element_type=F32
            )
            total = total + read * (gates[:, b + 1 : b + 2] * use)
            at += stretches // 2 ** (b + 1)
        return total

    scale = [digit.astype(F32) for digit in digits]

    def attend_pair(duo, chunk):
        for inner in range(per):
            head = chunk * per + inner
            for odd in range(2):
                token = pl.ds(pl.multiple_of((duo * 2 + odd) * C, C), C)
                comb[token, lanes(head)] = attend(duo, odd, head)
                query = q[token, lanes(head)].astype(F32)
                for level in range(ctx_bits):
                    at = bits + 1 + level
                    gate = gate_cols[head, token, at : at + 1] * scale[level]
                    gated[head, pl.ds(odd * C, C), slot(level)] = (query * gate).astype(BF16)

    def sib_copy(n, chunk):
        at = pl.ds(pl.multiple_of(chunk * per * width, per * width), per * width)
        return pltpu.make_async_remote_copy(
            src_ref=to_sib.at[n, :, at], dst_ref=from_sib.at[n, :, at],
            send_sem=n_send.at[n, chunk], recv_sem=n_recv.at[n, chunk],
            device_id=sib, device_id_type=MESH,
        )

    ones = jnp.full((width, width), 1.0 / width, BF16)

    def finish(duo, sub, chunk, dst):
        token = pl.ds(pl.multiple_of((duo * 2 + sub) * C, C), C)
        at = pl.ds(pl.multiple_of(sub * C, C), C)
        normed = []
        for inner in range(per):
            head = chunk * per + inner
            total = comb[token, lanes(head)] + jnp.dot(
                gated[head, at], r_buf[head], preferred_element_type=F32
            )
            mean = jnp.dot((total * total).astype(BF16), ones, preferred_element_type=F32)
            normed.append((total * lax.rsqrt(mean + EPS)).astype(BF16))
        dst[:, pl.ds(pl.multiple_of(chunk * per * width, per * width), per * width)] = jnp.concatenate(normed, axis=1)

    def p_copy(tile):
        return pltpu.make_async_remote_copy(
            src_ref=p_send.at[tile], dst_ref=p_recv.at[tile],
            send_sem=p_ssem.at[tile], recv_sem=p_rsem.at[tile],
            device_id=far_dev, device_id_type=MESH,
        )

    def project(n, part, tile):
        at = pl.ds(pl.multiple_of(tile * TILE, TILE), TILE)
        return jnp.dot((from_sib if part else mine)[n], w[part, :, at], preferred_element_type=F32)

    def handed(n):
        for level in range(2, ctx_bits):
            @pl.when(digits[level] == 1)
            def _():
                hand_copy(level, theirs(n)).wait_recv()

    def finish_chunk(n, duo, chunk):
        finish(duo, 1 - core, chunk, to_sib.at[n])
        sib_copy(n, chunk).start()
        finish(duo, core, chunk, mine.at[n])

    lags = [0 + 2 * level for level in range(ctx_bits)]
    counts = [CHUNKS if level < 2 else half for level in range(ctx_bits)]
    ready = max(CHUNKS, *[lag + half for lag in lags]) - half
    steps = max([CHUNKS, ready + half] + [lag + count for lag, count in zip(lags, counts)])

    early = 0
    for n in range(early):
        attend_pair(other, ours(n))

    @pl.loop(0, steps)
    def _(n):
        for level in reversed(range(ctx_bits)):
            at = n - lags[level]

            @pl.when((at >= 0) & (at < counts[level]))
            def _():
                service(level, at)

        @pl.when(n < CHUNKS - early)
        def _():
            attend_pair(other, ours(n + early))

        @pl.when((n >= ready) & (n < ready + half))
        def _():
            finish_chunk(0, other, ours(flip(n - ready)))

    @pl.loop(0, half)
    def _(n):
        handed(flip(n))
        finish_chunk(0, other, theirs(flip(n)))

    w_load.wait()

    @pl.loop(0, tiles)
    def _(tile):
        near_part = project(0, 0, tile)

        @pl.when(tile == 0)
        def _():
            for chunk in range(CHUNKS):
                sib_copy(0, chunk).wait_recv()

        w_copy(tile).wait_recv()
        p_send[tile] = (near_part + project(0, 1, tile)).astype(BF16)
        p_copy(tile).start()

    @pl.loop(0, CHUNKS)
    def _(chunk):
        attend_pair(pair, chunk)

    @pl.loop(0, CHUNKS)
    def _(chunk):
        finish_chunk(1, pair, chunk)

    for chunk in range(CHUNKS):
        sib_copy(1, chunk).wait_recv()

    @pl.loop(0, tiles)
    def _(tile):
        own[:, pl.ds(pl.multiple_of(tile * TILE, TILE), TILE)] = project(1, 0, tile) + project(1, 1, tile)

    @pl.loop(0, tiles)
    def _(tile):
        p_copy(tile).wait_send()
        w_copy(tile).wait_send()

    for n in range(2):
        for chunk in range(CHUNKS):
            sib_copy(n, chunk).wait_send()

    @pl.loop(0, CHUNKS)
    def _(chunk):
        state_copy(0, chunk).wait_send()

    for level in range(1, ctx_bits):
        @pl.when(wanted[level] == 1)
        def _():
            @pl.loop(0, counts[level])
            def _(n):
                @pl.when(((n < direct) | (skips == 1)) if level == 2 else n >= 0)
                def _():
                    state_copy(level, ours(n)).wait_send()

        if level == 2:
            @pl.when(skips == 1)
            def _():
                for n in range(direct, half):
                    over_copy(ours(n)).wait_send()

        if level > 1:
            @pl.when(digits[level] == 1)
            def _():
                @pl.loop(0, half)
                def _(n):
                    hand_copy(level, ours(n)).wait_send()

    @pl.loop(0, tiles)
    def _(tile):
        at = pl.ds(pl.multiple_of(tile * TILE, TILE), TILE)
        p_copy(tile).wait_recv()
        out[:, at] = (own[:, at] + p_recv[tile].astype(F32)).astype(BF16)


def on_device(query_rows, key_rows, value_rows, level_gate, out_weight):
    tokens, cols = query_rows.shape
    levels, heads, _ = level_gate.shape
    width = cols // heads
    model = out_weight.shape[1]
    rows = tokens // lax.axis_size("head")
    ctx_size = lax.axis_size("ctx")
    ctx_bits = ctx_size.bit_length() - 1
    tiles = model // TILE
    near = len(buckets_of(tokens // C))
    dma = pltpu.SemaphoreType.DMA
    flops = 2 * tokens * cols * (model + 2 * C + width * 7)
    operands = [
        pltpu.with_memory_space_constraint(x, pltpu.HBM)
        for x in (query_rows, key_rows, value_rows, level_gate, out_weight)
    ]
    return pl.pallas_call(
        functools.partial(kernel, ctx_size, heads, levels),
        out_shape=pltpu.VMEM((rows, model), BF16),
        in_specs=[pl.BlockSpec(memory_space=pl.ANY)] * 5,
        out_specs=pl.BlockSpec(memory_space=pltpu.VMEM),
        scratch_shapes=[
            pltpu.VMEM((tokens, cols), BF16),
            pltpu.VMEM((tokens, cols), BF16),
            pltpu.VMEM((tokens, cols), BF16),
            pltpu.VMEM((levels, heads, tokens), F32),
            pltpu.VMEM((heads, tokens, -(-levels // 8) * 8), F32),
            pltpu.VMEM((2, cols, model), BF16),
            pltpu.VMEM((tokens, cols), F32),
            pltpu.VMEM((heads, width, width), F32),
            pltpu.VMEM((heads, near, width, width), BF16),
            pltpu.VMEM((ctx_bits, heads, width, width), BF16),
            pltpu.VMEM((heads, ctx_bits * width, width), BF16),
            pltpu.VMEM((heads, 2 * C, ctx_bits * width), BF16),
            pltpu.VMEM((2, rows, cols), BF16),
            pltpu.VMEM((2, rows, cols), BF16),
            pltpu.VMEM((2, rows, cols), BF16),
            pltpu.VMEM((tiles, rows, TILE), BF16),
            pltpu.VMEM((tiles, rows, TILE), BF16),
            pltpu.VMEM((rows, model), F32),
            dma((7,)),
            dma((ctx_bits, CHUNKS)),
            dma((ctx_bits, CHUNKS)),
            dma((ctx_bits, CHUNKS)),
            dma((CHUNKS,)),
            dma((tiles,)),
            dma((tiles,)),
            dma((2, CHUNKS)),
            dma((2, CHUNKS)),
            dma((tiles,)),
            dma((tiles,)),
        ],
        compiler_params=pltpu.CompilerParams(
            collective_id=0, has_side_effects=True, vmem_limit_bytes=54 * 1024 * 1024
        ),
        cost_estimate=pl.CostEstimate(
            flops=flops, bytes_accessed=20 * 1024 * 1024, transcendentals=tokens * heads
        ),
        name="levels_project",
    )(*operands)


def solution(mesh):
    in_specs = (
        P("ctx", "head"),
        P("ctx", "head"),
        P("ctx", "head"),
        P(None, "head", "ctx"),
        P("head", None),
    )
    out_specs = P(("ctx", "head"), None)
    return jax.shard_map(
        on_device, mesh=mesh, in_specs=in_specs, out_specs=out_specs, check_vma=False
    )
```

```python
import functools

import jax
import jax.numpy as jnp
from jax import lax
from jax.experimental import pallas as pl
from jax.experimental.pallas import tpu as pltpu
from jax.sharding import PartitionSpec as P

C = 256
EPS = 1e-06
CHUNKS = 8
GROUPS = 4
TILE = 512
MESH = pl.DeviceIdType.MESH
F32 = jnp.float32
BF16 = jnp.bfloat16


def buckets_of(stretches):
    keys = []
    span = 1
    while span < stretches:
        keys += [(span, block) for block in range(0, stretches // span, 2)]
        span *= 2
    return keys


def kernel(
    ctx_size, heads, levels,
    q_hbm, k_hbm, v_hbm, g_hbm, w_hbm, out,
    q, k, v, g, gate_cols, w, comb, run, near, s_buf, r_buf, gated,
    to_sib, from_sib, mine, p_send, p_recv, own,
    load_sem, st_send, st_recv, hand_send, over_send, w_send, w_recv, n_send, n_recv, p_ssem, p_rsem,
):
    ctx_bits = ctx_size.bit_length() - 1
    tokens, width = q.shape[0], q.shape[1] // heads
    stretches = tokens // C
    bits = stretches.bit_length() - 1
    per = heads // CHUNKS
    half = CHUNKS // 2
    wide = heads // GROUPS
    ratio = CHUNKS // GROUPS
    half_groups = GROUPS // 2
    rows = own.shape[0]
    tiles = p_send.shape[0]
    keys = buckets_of(stretches)
    me = lax.axis_index("ctx")
    head_at = lax.axis_index("head")
    digits = [lax.rem(lax.div(me, 2**b), 2) for b in range(ctx_bits)]
    ahead = me + 2
    has_next = (ahead < ctx_size).astype(jnp.int32)
    has_prev = (me >= 2).astype(jnp.int32)
    wanted = [lax.rem(lax.div(ahead, 2**b), 2) * has_next for b in range(ctx_bits)]
    skips = digits[1] * (1 - digits[2]) if ctx_bits > 2 else jnp.int32(0)
    skipped = digits[1] * digits[2] if ctx_bits > 2 else jnp.int32(0)
    over, under = {"ctx": me + 4}, {"ctx": me - 4}
    partner = {"ctx": me + 1 - 2 * digits[0]}
    nxt, prev = {"ctx": ahead}, {"ctx": me - 2}
    core = lax.rem(head_at, 2)
    pair = lax.div(head_at, 2)
    other = 1 - pair
    sib = {"head": pair * 2 + 1 - core}
    far_dev = {"head": other * 2 + core}

    barrier = pltpu.get_barrier_semaphore()
    for device in (partner, sib, far_dev):
        pl.semaphore_signal(barrier, inc=1, device_id=device, device_id_type=MESH)

    @pl.when(has_next == 1)
    def _():
        pl.semaphore_signal(barrier, inc=1, device_id=nxt, device_id_type=MESH)

    @pl.when(has_prev == 1)
    def _():
        pl.semaphore_signal(barrier, inc=1, device_id=prev, device_id_type=MESH)

    @pl.when(skips == 1)
    def _():
        pl.semaphore_signal(barrier, inc=1, device_id=over, device_id_type=MESH)

    @pl.when(skipped == 1)
    def _():
        pl.semaphore_signal(barrier, inc=1, device_id=under, device_id_type=MESH)

    cols = q.shape[1]
    part_cols = cols // 2

    def half_copy(src, dst, which, sem):
        at = pl.ds(pl.multiple_of(which * part_cols, part_cols), part_cols)
        return pltpu.make_async_copy(src.at[:, at], dst.at[:, at], load_sem.at[sem])

    first = 1 - digits[0]
    kv_loads = [
        [half_copy(k_hbm, k, first, 0), half_copy(v_hbm, v, first, 1)],
        [half_copy(k_hbm, k, digits[0], 2), half_copy(v_hbm, v, digits[0], 3)],
    ]
    q_load = pltpu.make_async_copy(q_hbm, q, load_sem.at[4])
    g_load = pltpu.make_async_copy(g_hbm, g, load_sem.at[5])
    w_load = pltpu.make_async_copy(w_hbm, w.at[0], load_sem.at[6])
    for copy in kv_loads[0] + kv_loads[1] + [q_load, g_load]:
        copy.start()

    def w_copy(tile):
        at = pl.ds(pl.multiple_of(tile * TILE, TILE), TILE)
        return pltpu.make_async_remote_copy(
            src_ref=w_hbm.at[:, at], dst_ref=w.at[1, :, at],
            send_sem=w_send.at[tile], recv_sem=w_recv.at[tile],
            device_id=sib, device_id_type=MESH,
        )

    def slot(level):
        return pl.ds(level * width, width)

    def group(chunk):
        return pl.ds(chunk * per, per)

    def state_copy(level, chunk, relay=False):
        came = r_buf.at[group(chunk), slot(level)]
        return pltpu.make_async_remote_copy(
            src_ref=came if relay else s_buf.at[level, group(chunk)], dst_ref=came,
            send_sem=st_send.at[level, chunk], recv_sem=st_recv.at[level, chunk],
            device_id=nxt if level else partner, device_id_type=MESH,
        )

    direct = half // 2

    def over_copy(chunk):
        return pltpu.make_async_remote_copy(
            src_ref=s_buf.at[2, group(chunk)], dst_ref=r_buf.at[group(chunk), slot(2)],
            send_sem=over_send.at[chunk], recv_sem=st_recv.at[2, chunk],
            device_id=over, device_id_type=MESH,
        )

    def flip(n):
        return lax.rem(n + skipped * direct, half)

    def flip_group(n):
        return lax.rem(n + skipped * (half_groups // 2), half_groups)

    def hand_copy(level, chunk):
        came = r_buf.at[group(chunk), slot(level)]
        return pltpu.make_async_remote_copy(
            src_ref=came, dst_ref=came,
            send_sem=hand_send.at[level, chunk], recv_sem=st_recv.at[level, chunk],
            device_id=partner, device_id_type=MESH,
        )

    def ours(n):
        return lax.rem(n + digits[0] * half, CHUNKS)

    def theirs(n):
        return lax.rem(n + (1 - digits[0]) * half, CHUNKS)

    def our_group(n):
        return lax.rem(n + digits[0] * half_groups, GROUPS)

    def their_group(n):
        return lax.rem(n + (1 - digits[0]) * half_groups, GROUPS)

    def pass_on(level, chunk, n):
        if level < ctx_bits:
            @pl.when((digits[level] == 0) & (wanted[level] == 1))
            def _():
                s_buf[level, group(chunk)] = run[group(chunk)].astype(BF16)
                if level == 2:
                    @pl.when(n >= direct)
                    def _():
                        over_copy(chunk).start()

                state_copy(level, chunk).start()

    def service(level, n):
        if level == 2:
            n = flip(n)
        chunk = ours(n)
        if level == 0:
            state_copy(0, chunk).wait_recv()
            if ctx_bits > 1:
                run[group(chunk)] = run[group(chunk)] + r_buf[group(chunk), slot(0)].astype(F32)
                pass_on(1, chunk, n)
            return

        @pl.when(digits[level] == 1)
        def _():
            state_copy(level, chunk).wait_recv()
            if level > 1:
                @pl.when((wanted[level] == 1) & ((n < direct) if level == 2 else True))
                def _():
                    state_copy(level, chunk, relay=True).start()

                hand_copy(level, chunk).start()
            if level + 1 < ctx_bits:
                @pl.when(n < half)
                def _():
                    run[group(chunk)] = run[group(chunk)] + r_buf[group(chunk), slot(level)].astype(F32)
                    pass_on(level + 1, chunk, n)

    def lanes(head):
        return pl.ds(pl.multiple_of(head * width, width), width)

    def states(chunk):
        for inner in range(wide):
            head = chunk * wide + inner
            col = lanes(head)
            sums = {}
            for c in range(stretches):
                token = pl.ds(c * C, C)
                sums[1, c] = lax.dot_general(
                    k[token, col], v[token, col], (((0,), (0,)), ((), ())),
                    preferred_element_type=F32,
                )
            span = 1
            while span < stretches:
                for block in range(stretches // span // 2):
                    sums[span * 2, block] = sums[span, block * 2] + sums[span, block * 2 + 1]
                span *= 2
            for n, key in enumerate(keys):
                near[head, n] = sums[key].astype(BF16)
            run[head] = sums[stretches, 0]
            s_buf[0, head] = sums[stretches, 0].astype(BF16)

    for copy in kv_loads[0]:
        copy.wait()

    @pl.loop(0, half_groups)
    def _(n):
        states(their_group(n))

    pl.semaphore_wait(barrier, 3 + has_next + has_prev + skips + skipped)

    @pl.loop(0, half)
    def _(n):
        state_copy(0, theirs(n)).start()

    for copy in kv_loads[1]:
        copy.wait()

    @pl.loop(half_groups, GROUPS)
    def _(n):
        states(their_group(n))
        for inner in range(ratio):
            state_copy(0, theirs(n * ratio + inner)).start()

    @pl.loop(0, tiles)
    def _(tile):
        w_copy(tile).start()

    w_load.start()
    for level in range(1, ctx_bits):
        @pl.when(digits[level] == 0)
        def _():
            for head in range(heads):
                r_buf[head, slot(level)] = jnp.zeros((width, width), BF16)

    q_load.wait()
    g_load.wait()
    pad = gate_cols.shape[2] - levels
    for head in range(heads):
        strips = [g[level, head : head + 1, :] for level in range(levels)]
        if pad:
            strips.append(jnp.zeros((pad, tokens), F32))
        gate_cols[head] = jnp.concatenate(strips, axis=0).T

    keep = lax.broadcasted_iota(jnp.int32, (C, C), 0) >= lax.broadcasted_iota(
        jnp.int32, (C, C), 1
    )

    def attend(duo, odd, head):
        block = duo * 2 + odd
        token = pl.ds(pl.multiple_of(block * C, C), C)
        col = lanes(head)
        gates = gate_cols[head, token, :]
        query = q[token, col]
        scores = lax.dot_general(
            query, k[token, col], (((1,), (1,)), ((), ())), preferred_element_type=F32
        )
        weights = (jnp.where(keep, scores, 0.0) * gates[:, 0:1]).astype(BF16)
        total = jnp.dot(weights, v[token, col], preferred_element_type=F32)
        if odd:
            read = jnp.dot(query, near[head, duo], preferred_element_type=F32)
            total = total + read * gates[:, 1:2]
        at = stretches // 2
        for b in range(1, bits):
            span = lax.div(duo, 2 ** (b - 1))
            use = lax.rem(span, 2).astype(F32)
            read = jnp.dot(
                query, near[head, at + lax.div(span, 2)], preferred_element_type=F32
            )
            total = total + read * (gates[:, b + 1 : b + 2] * use)
            at += stretches // 2 ** (b + 1)
        return total

    scale = [digit.astype(F32) for digit in digits]

    def attend_pair(duo, chunk):
        for inner in range(wide):
            head = chunk * wide + inner
            for odd in range(2):
                token = pl.ds(pl.multiple_of((duo * 2 + odd) * C, C), C)
                comb[token, lanes(head)] = attend(duo, odd, head)
                query = q[token, lanes(head)].astype(F32)
                for level in range(ctx_bits):
                    at = bits + 1 + level
                    gate = gate_cols[head, token, at : at + 1] * scale[level]
                    gated[head, pl.ds(odd * C, C), slot(level)] = (query * gate).astype(BF16)

    def sib_copy(n, chunk):
        at = pl.ds(pl.multiple_of(chunk * wide * width, wide * width), wide * width)
        return pltpu.make_async_remote_copy(
            src_ref=to_sib.at[n, :, at], dst_ref=from_sib.at[n, :, at],
            send_sem=n_send.at[n, chunk], recv_sem=n_recv.at[n, chunk],
            device_id=sib, device_id_type=MESH,
        )

    ones = jnp.full((width, width), 1.0 / width, BF16)

    def finish(duo, sub, chunk, dst):
        token = pl.ds(pl.multiple_of((duo * 2 + sub) * C, C), C)
        at = pl.ds(pl.multiple_of(sub * C, C), C)
        normed = []
        for inner in range(wide):
            head = chunk * wide + inner
            total = comb[token, lanes(head)] + jnp.dot(
                gated[head, at], r_buf[head], preferred_element_type=F32
            )
            mean = jnp.dot((total * total).astype(BF16), ones, preferred_element_type=F32)
            normed.append((total * lax.rsqrt(mean + EPS)).astype(BF16))
        dst[:, pl.ds(pl.multiple_of(chunk * wide * width, wide * width), wide * width)] = jnp.concatenate(normed, axis=1)

    def p_copy(tile):
        return pltpu.make_async_remote_copy(
            src_ref=p_send.at[tile], dst_ref=p_recv.at[tile],
            send_sem=p_ssem.at[tile], recv_sem=p_rsem.at[tile],
            device_id=far_dev, device_id_type=MESH,
        )

    def project(n, part, tile):
        at = pl.ds(pl.multiple_of(tile * TILE, TILE), TILE)
        return jnp.dot((from_sib if part else mine)[n], w[part, :, at], preferred_element_type=F32)

    def handed(n):
        for level in range(2, ctx_bits):
            @pl.when(digits[level] == 1)
            def _():
                hand_copy(level, theirs(n)).wait_recv()

    def finish_chunk(n, duo, chunk):
        finish(duo, 1 - core, chunk, to_sib.at[n])
        sib_copy(n, chunk).start()
        finish(duo, core, chunk, mine.at[n])

    lags = [0 + 4 * level for level in range(ctx_bits)]
    counts = [CHUNKS if level < 2 else half for level in range(ctx_bits)]
    wait = 2
    ready = max(wait + CHUNKS, *[lag + half for lag in lags]) - half + ratio - 1
    steps = max([wait + CHUNKS, ready + half] + [lag + count for lag, count in zip(lags, counts)])

    late = wait * has_next

    @pl.loop(0, steps)
    def _(n):
        for level in reversed(range(ctx_bits)):
            at = n - lags[level]

            @pl.when((at >= 0) & (at < counts[level]))
            def _():
                service(level, at)

        @pl.when((n >= late) & (n < late + CHUNKS) & (lax.rem(n - late, ratio) == 0))
        def _():
            attend_pair(other, our_group(lax.div(n - late, ratio)))

        @pl.when((n >= ready) & (n < ready + half) & (lax.rem(n - ready, ratio) == 0))
        def _():
            finish_chunk(0, other, our_group(flip_group(lax.div(n - ready, ratio))))

    @pl.loop(0, half_groups)
    def _(n):
        for inner in range(ratio):
            handed(flip_group(n) * ratio + inner)
        finish_chunk(0, other, their_group(flip_group(n)))

    w_load.wait()

    @pl.loop(0, tiles)
    def _(tile):
        near_part = project(0, 0, tile)

        @pl.when(tile == 0)
        def _():
            for chunk in range(GROUPS):
                sib_copy(0, chunk).wait_recv()

        w_copy(tile).wait_recv()
        p_send[tile] = (near_part + project(0, 1, tile)).astype(BF16)
        p_copy(tile).start()

    @pl.loop(0, GROUPS)
    def _(chunk):
        attend_pair(pair, chunk)

    @pl.loop(0, GROUPS)
    def _(chunk):
        finish_chunk(1, pair, chunk)

    for chunk in range(GROUPS):
        sib_copy(1, chunk).wait_recv()

    @pl.loop(0, tiles)
    def _(tile):
        own[:, pl.ds(pl.multiple_of(tile * TILE, TILE), TILE)] = project(1, 0, tile) + project(1, 1, tile)

    @pl.loop(0, tiles)
    def _(tile):
        p_copy(tile).wait_send()
        w_copy(tile).wait_send()

    for n in range(2):
        for chunk in range(GROUPS):
            sib_copy(n, chunk).wait_send()

    @pl.loop(0, CHUNKS)
    def _(chunk):
        state_copy(0, chunk).wait_send()

    for level in range(1, ctx_bits):
        @pl.when(wanted[level] == 1)
        def _():
            @pl.loop(0, counts[level])
            def _(n):
                @pl.when(((n < direct) | (skips == 1)) if level == 2 else n >= 0)
                def _():
                    state_copy(level, ours(n)).wait_send()

        if level == 2:
            @pl.when(skips == 1)
            def _():
                for n in range(direct, half):
                    over_copy(ours(n)).wait_send()

        if level > 1:
            @pl.when(digits[level] == 1)
            def _():
                @pl.loop(0, half)
                def _(n):
                    hand_copy(level, ours(n)).wait_send()

    @pl.loop(0, tiles)
    def _(tile):
        at = pl.ds(pl.multiple_of(tile * TILE, TILE), TILE)
        p_copy(tile).wait_recv()
        out[:, at] = (own[:, at] + p_recv[tile].astype(F32)).astype(BF16)


def on_device(query_rows, key_rows, value_rows, level_gate, out_weight):
    tokens, cols = query_rows.shape
    levels, heads, _ = level_gate.shape
    width = cols // heads
    model = out_weight.shape[1]
    rows = tokens // lax.axis_size("head")
    ctx_size = lax.axis_size("ctx")
    ctx_bits = ctx_size.bit_length() - 1
    tiles = model // TILE
    near = len(buckets_of(tokens // C))
    dma = pltpu.SemaphoreType.DMA
    flops = 2 * tokens * cols * (model + 2 * C + width * 7)
    operands = [
        pltpu.with_memory_space_constraint(x, pltpu.HBM)
        for x in (query_rows, key_rows, value_rows, level_gate, out_weight)
    ]
    return pl.pallas_call(
        functools.partial(kernel, ctx_size, heads, levels),
        out_shape=pltpu.VMEM((rows, model), BF16),
        in_specs=[pl.BlockSpec(memory_space=pl.ANY)] * 5,
        out_specs=pl.BlockSpec(memory_space=pltpu.VMEM),
        scratch_shapes=[
            pltpu.VMEM((tokens, cols), BF16),
            pltpu.VMEM((tokens, cols), BF16),
            pltpu.VMEM((tokens, cols), BF16),
            pltpu.VMEM((levels, heads, tokens), F32),
            pltpu.VMEM((heads, tokens, -(-levels // 8) * 8), F32),
            pltpu.VMEM((2, cols, model), BF16),
            pltpu.VMEM((tokens, cols), F32),
            pltpu.VMEM((heads, width, width), F32),
            pltpu.VMEM((heads, near, width, width), BF16),
            pltpu.VMEM((ctx_bits, heads, width, width), BF16),
            pltpu.VMEM((heads, ctx_bits * width, width), BF16),
            pltpu.VMEM((heads, 2 * C, ctx_bits * width), BF16),
            pltpu.VMEM((2, rows, cols), BF16),
            pltpu.VMEM((2, rows, cols), BF16),
            pltpu.VMEM((2, rows, cols), BF16),
            pltpu.VMEM((tiles, rows, TILE), BF16),
            pltpu.VMEM((tiles, rows, TILE), BF16),
            pltpu.VMEM((rows, model), F32),
            dma((7,)),
            dma((ctx_bits, CHUNKS)),
            dma((ctx_bits, CHUNKS)),
            dma((ctx_bits, CHUNKS)),
            dma((CHUNKS,)),
            dma((tiles,)),
            dma((tiles,)),
            dma((2, GROUPS)),
            dma((2, GROUPS)),
            dma((tiles,)),
            dma((tiles,)),
        ],
        compiler_params=pltpu.CompilerParams(
            collective_id=0, has_side_effects=True, vmem_limit_bytes=54 * 1024 * 1024
        ),
        cost_estimate=pl.CostEstimate(
            flops=flops, bytes_accessed=20 * 1024 * 1024, transcendentals=tokens * heads
        ),
        name="levels_project",
    )(*operands)


def solution(mesh):
    in_specs = (
        P("ctx", "head"),
        P("ctx", "head"),
        P("ctx", "head"),
        P(None, "head", "ctx"),
        P("head", None),
    )
    out_specs = P(("ctx", "head"), None)
    return jax.shard_map(
        on_device, mesh=mesh, in_specs=in_specs, out_specs=out_specs, check_vma=False
    )
```

```python
import functools

import jax
import jax.numpy as jnp
from jax import lax
from jax.experimental import pallas as pl
from jax.experimental.pallas import tpu as pltpu
from jax.sharding import PartitionSpec as P

C = 256
EPS = 1e-06
CHUNKS = 8
GROUPS = 4
TILE = 512
MESH = pl.DeviceIdType.MESH
F32 = jnp.float32
BF16 = jnp.bfloat16


def buckets_of(stretches):
    keys = []
    span = 1
    while span < stretches:
        keys += [(span, block) for block in range(0, stretches // span, 2)]
        span *= 2
    return keys


def kernel(
    ctx_size, heads, levels,
    q_hbm, k_hbm, v_hbm, g_hbm, w_hbm, out,
    q, k, v, g, gate_cols, w, comb, run, near, s_buf, r_buf, gated,
    to_sib, from_sib, mine, p_send, p_recv, own,
    load_sem, st_send, st_recv, hand_send, over_send, w_send, w_recv, n_send, n_recv, p_ssem, p_rsem,
):
    ctx_bits = ctx_size.bit_length() - 1
    tokens, width = q.shape[0], q.shape[1] // heads
    stretches = tokens // C
    bits = stretches.bit_length() - 1
    per = heads // CHUNKS
    half = CHUNKS // 2
    wide = heads // GROUPS
    ratio = CHUNKS // GROUPS
    half_groups = GROUPS // 2
    rows = own.shape[0]
    tiles = p_send.shape[0]
    keys = buckets_of(stretches)
    me = lax.axis_index("ctx")
    head_at = lax.axis_index("head")
    digits = [lax.rem(lax.div(me, 2**b), 2) for b in range(ctx_bits)]
    ahead = me + 2
    has_next = (ahead < ctx_size).astype(jnp.int32)
    has_prev = (me >= 2).astype(jnp.int32)
    wanted = [lax.rem(lax.div(ahead, 2**b), 2) * has_next for b in range(ctx_bits)]
    skips = digits[1] * (1 - digits[2]) if ctx_bits > 2 else jnp.int32(0)
    skipped = digits[1] * digits[2] if ctx_bits > 2 else jnp.int32(0)
    over, under = {"ctx": me + 4}, {"ctx": me - 4}
    partner = {"ctx": me + 1 - 2 * digits[0]}
    nxt, prev = {"ctx": ahead}, {"ctx": me - 2}
    core = lax.rem(head_at, 2)
    pair = lax.div(head_at, 2)
    other = 1 - pair
    sib = {"head": pair * 2 + 1 - core}
    far_dev = {"head": other * 2 + core}

    barrier = pltpu.get_barrier_semaphore()
    for device in (partner, sib, far_dev):
        pl.semaphore_signal(barrier, inc=1, device_id=device, device_id_type=MESH)

    @pl.when(has_next == 1)
    def _():
        pl.semaphore_signal(barrier, inc=1, device_id=nxt, device_id_type=MESH)

    @pl.when(has_prev == 1)
    def _():
        pl.semaphore_signal(barrier, inc=1, device_id=prev, device_id_type=MESH)

    @pl.when(skips == 1)
    def _():
        pl.semaphore_signal(barrier, inc=1, device_id=over, device_id_type=MESH)

    @pl.when(skipped == 1)
    def _():
        pl.semaphore_signal(barrier, inc=1, device_id=under, device_id_type=MESH)

    cols = q.shape[1]
    part_cols = cols // 2

    def half_copy(src, dst, which, sem):
        at = pl.ds(pl.multiple_of(which * part_cols, part_cols), part_cols)
        return pltpu.make_async_copy(src.at[:, at], dst.at[:, at], load_sem.at[sem])

    first = 1 - digits[0]
    kv_loads = [
        [half_copy(k_hbm, k, first, 0), half_copy(v_hbm, v, first, 1)],
        [half_copy(k_hbm, k, digits[0], 2), half_copy(v_hbm, v, digits[0], 3)],
    ]
    q_load = pltpu.make_async_copy(q_hbm, q, load_sem.at[4])
    g_load = pltpu.make_async_copy(g_hbm, g, load_sem.at[5])
    w_load = pltpu.make_async_copy(w_hbm, w.at[0], load_sem.at[6])
    for copy in kv_loads[0] + kv_loads[1] + [q_load, g_load]:
        copy.start()

    def w_copy(tile):
        at = pl.ds(pl.multiple_of(tile * TILE, TILE), TILE)
        return pltpu.make_async_remote_copy(
            src_ref=w_hbm.at[:, at], dst_ref=w.at[1, :, at],
            send_sem=w_send.at[tile], recv_sem=w_recv.at[tile],
            device_id=sib, device_id_type=MESH,
        )

    def slot(level):
        return pl.ds(level * width, width)

    def group(chunk):
        return pl.ds(chunk * per, per)

    def state_copy(level, chunk, relay=False):
        came = r_buf.at[group(chunk), slot(level)]
        return pltpu.make_async_remote_copy(
            src_ref=came if relay else s_buf.at[level, group(chunk)], dst_ref=came,
            send_sem=st_send.at[level, chunk], recv_sem=st_recv.at[level, chunk],
            device_id=nxt if level else partner, device_id_type=MESH,
        )

    direct = half // 2

    def over_copy(chunk):
        return pltpu.make_async_remote_copy(
            src_ref=s_buf.at[2, group(chunk)], dst_ref=r_buf.at[group(chunk), slot(2)],
            send_sem=over_send.at[chunk], recv_sem=st_recv.at[2, chunk],
            device_id=over, device_id_type=MESH,
        )

    def flip(n):
        return lax.rem(n + skipped * direct, half)

    def flip_group(n):
        return lax.rem(n + skipped * (half_groups // 2), half_groups)

    def hand_copy(level, chunk):
        came = r_buf.at[group(chunk), slot(level)]
        return pltpu.make_async_remote_copy(
            src_ref=came, dst_ref=came,
            send_sem=hand_send.at[level, chunk], recv_sem=st_recv.at[level, chunk],
            device_id=partner, device_id_type=MESH,
        )

    def ours(n):
        return lax.rem(n + digits[0] * half, CHUNKS)

    def theirs(n):
        return lax.rem(n + (1 - digits[0]) * half, CHUNKS)

    def our_group(n):
        return lax.rem(n + digits[0] * half_groups, GROUPS)

    def their_group(n):
        return lax.rem(n + (1 - digits[0]) * half_groups, GROUPS)

    def pass_on(level, chunk, n):
        if level < ctx_bits:
            @pl.when((digits[level] == 0) & (wanted[level] == 1))
            def _():
                s_buf[level, group(chunk)] = run[group(chunk)].astype(BF16)
                if level == 2:
                    @pl.when(n >= direct)
                    def _():
                        over_copy(chunk).start()

                state_copy(level, chunk).start()

    def service(level, n):
        if level == 2:
            n = flip(n)
        chunk = ours(n)
        if level == 0:
            state_copy(0, chunk).wait_recv()
            if ctx_bits > 1:
                run[group(chunk)] = run[group(chunk)] + r_buf[group(chunk), slot(0)].astype(F32)
                pass_on(1, chunk, n)
            return

        @pl.when(digits[level] == 1)
        def _():
            state_copy(level, chunk).wait_recv()
            if level > 1:
                @pl.when((wanted[level] == 1) & ((n < direct) if level == 2 else True))
                def _():
                    state_copy(level, chunk, relay=True).start()

                hand_copy(level, chunk).start()
            if level + 1 < ctx_bits:
                @pl.when(n < half)
                def _():
                    run[group(chunk)] = run[group(chunk)] + r_buf[group(chunk), slot(level)].astype(F32)
                    pass_on(level + 1, chunk, n)

    def lanes(head):
        return pl.ds(pl.multiple_of(head * width, width), width)

    def states(chunk):
        for inner in range(wide):
            head = chunk * wide + inner
            col = lanes(head)
            sums = {}
            for c in range(stretches):
                token = pl.ds(c * C, C)
                sums[1, c] = lax.dot_general(
                    k[token, col], v[token, col], (((0,), (0,)), ((), ())),
                    preferred_element_type=F32,
                )
            span = 1
            while span < stretches:
                for block in range(stretches // span // 2):
                    sums[span * 2, block] = sums[span, block * 2] + sums[span, block * 2 + 1]
                span *= 2
            for n, key in enumerate(keys):
                near[head, n] = sums[key].astype(BF16)
            run[head] = sums[stretches, 0]
            s_buf[0, head] = sums[stretches, 0].astype(BF16)

    for copy in kv_loads[0]:
        copy.wait()

    @pl.loop(0, half_groups)
    def _(n):
        states(their_group(n))

    pl.semaphore_wait(barrier, 3 + has_next + has_prev + skips + skipped)

    @pl.loop(0, half)
    def _(n):
        state_copy(0, theirs(n)).start()

    for copy in kv_loads[1]:
        copy.wait()

    @pl.loop(half_groups, GROUPS)
    def _(n):
        states(their_group(n))
        for inner in range(ratio):
            state_copy(0, theirs(n * ratio + inner)).start()

    @pl.loop(0, tiles)
    def _(tile):
        w_copy(tile).start()

    w_load.start()
    for level in range(1, ctx_bits):
        @pl.when(digits[level] == 0)
        def _():
            for head in range(heads):
                r_buf[head, slot(level)] = jnp.zeros((width, width), BF16)

    q_load.wait()
    g_load.wait()
    pad = gate_cols.shape[2] - levels
    for head in range(heads):
        strips = [g[level, head : head + 1, :] for level in range(levels)]
        if pad:
            strips.append(jnp.zeros((pad, tokens), F32))
        gate_cols[head] = jnp.concatenate(strips, axis=0).T

    keep = lax.broadcasted_iota(jnp.int32, (C, C), 0) >= lax.broadcasted_iota(
        jnp.int32, (C, C), 1
    )

    def attend(duo, odd, head):
        block = duo * 2 + odd
        token = pl.ds(pl.multiple_of(block * C, C), C)
        col = lanes(head)
        gates = gate_cols[head, token, :]
        query = q[token, col]
        scores = lax.dot_general(
            query, k[token, col], (((1,), (1,)), ((), ())), preferred_element_type=F32
        )
        weights = (jnp.where(keep, scores, 0.0) * gates[:, 0:1]).astype(BF16)
        total = jnp.dot(weights, v[token, col], preferred_element_type=F32)
        if odd:
            read = jnp.dot(query, near[head, duo], preferred_element_type=F32)
            total = total + read * gates[:, 1:2]
        at = stretches // 2
        for b in range(1, bits):
            span = lax.div(duo, 2 ** (b - 1))
            use = lax.rem(span, 2).astype(F32)
            read = jnp.dot(
                query, near[head, at + lax.div(span, 2)], preferred_element_type=F32
            )
            total = total + read * (gates[:, b + 1 : b + 2] * use)
            at += stretches // 2 ** (b + 1)
        return total

    scale = [digit.astype(F32) for digit in digits]

    def attend_pair(duo, chunk):
        for inner in range(wide):
            head = chunk * wide + inner
            for odd in range(2):
                token = pl.ds(pl.multiple_of((duo * 2 + odd) * C, C), C)
                comb[token, lanes(head)] = attend(duo, odd, head)
                query = q[token, lanes(head)].astype(F32)
                for level in range(ctx_bits):
                    at = bits + 1 + level
                    gate = gate_cols[head, token, at : at + 1] * scale[level]
                    gated[head, pl.ds(odd * C, C), slot(level)] = (query * gate).astype(BF16)

    def sib_copy(n, chunk):
        at = pl.ds(pl.multiple_of(chunk * wide * width, wide * width), wide * width)
        return pltpu.make_async_remote_copy(
            src_ref=to_sib.at[n, :, at], dst_ref=from_sib.at[n, :, at],
            send_sem=n_send.at[n, chunk], recv_sem=n_recv.at[n, chunk],
            device_id=sib, device_id_type=MESH,
        )

    ones = jnp.full((width, width), 1.0 / width, BF16)

    def finish(duo, sub, chunk, dst):
        token = pl.ds(pl.multiple_of((duo * 2 + sub) * C, C), C)
        at = pl.ds(pl.multiple_of(sub * C, C), C)
        for inner in range(wide):
            head = chunk * wide + inner
            total = comb[token, lanes(head)] + jnp.dot(
                gated[head, at], r_buf[head], preferred_element_type=F32
            )
            mean = jnp.dot((total * total).astype(BF16), ones, preferred_element_type=F32)
            dst[:, lanes(head)] = (total * lax.rsqrt(mean + EPS)).astype(BF16)

    def p_copy(tile):
        return pltpu.make_async_remote_copy(
            src_ref=p_send.at[tile], dst_ref=p_recv.at[tile],
            send_sem=p_ssem.at[tile], recv_sem=p_rsem.at[tile],
            device_id=far_dev, device_id_type=MESH,
        )

    def project(n, part, tile):
        at = pl.ds(pl.multiple_of(tile * TILE, TILE), TILE)
        return jnp.dot((from_sib if part else mine)[n], w[part, :, at], preferred_element_type=F32)

    def handed(n):
        for level in range(2, ctx_bits):
            @pl.when(digits[level] == 1)
            def _():
                hand_copy(level, theirs(n)).wait_recv()

    def finish_chunk(n, duo, chunk):
        finish(duo, 1 - core, chunk, to_sib.at[n])
        sib_copy(n, chunk).start()
        finish(duo, core, chunk, mine.at[n])

    lags = [0 + 4 * level for level in range(ctx_bits)]
    counts = [CHUNKS if level < 2 else half for level in range(ctx_bits)]
    wait = 1
    ready = max(wait + CHUNKS, *[lag + half for lag in lags]) - half + ratio - 1
    steps = max([wait + CHUNKS, ready + half] + [lag + count for lag, count in zip(lags, counts)])

    late = wait * has_next

    @pl.loop(0, steps)
    def _(n):
        for level in reversed(range(ctx_bits)):
            at = n - lags[level]

            @pl.when((at >= 0) & (at < counts[level]))
            def _():
                service(level, at)

        @pl.when((n >= late) & (n < late + CHUNKS) & (lax.rem(n - late, ratio) == 0))
        def _():
            attend_pair(other, our_group(lax.div(n - late, ratio)))

        @pl.when((n >= ready) & (n < ready + half) & (lax.rem(n - ready, ratio) == 0))
        def _():
            finish_chunk(0, other, our_group(flip_group(lax.div(n - ready, ratio))))

    @pl.loop(0, half_groups)
    def _(n):
        for inner in range(ratio):
            handed(flip_group(n) * ratio + inner)
        finish_chunk(0, other, their_group(flip_group(n)))

    w_load.wait()

    @pl.loop(0, tiles)
    def _(tile):
        near_part = project(0, 0, tile)

        @pl.when(tile == 0)
        def _():
            for chunk in range(GROUPS):
                sib_copy(0, chunk).wait_recv()

        w_copy(tile).wait_recv()
        p_send[tile] = (near_part + project(0, 1, tile)).astype(BF16)
        p_copy(tile).start()

    @pl.loop(0, GROUPS)
    def _(chunk):
        attend_pair(pair, chunk)

    @pl.loop(0, GROUPS)
    def _(chunk):
        finish_chunk(1, pair, chunk)

    for chunk in range(GROUPS):
        sib_copy(1, chunk).wait_recv()

    @pl.loop(0, tiles)
    def _(tile):
        own[:, pl.ds(pl.multiple_of(tile * TILE, TILE), TILE)] = project(1, 0, tile) + project(1, 1, tile)

    @pl.loop(0, tiles)
    def _(tile):
        p_copy(tile).wait_send()
        w_copy(tile).wait_send()

    for n in range(2):
        for chunk in range(GROUPS):
            sib_copy(n, chunk).wait_send()

    @pl.loop(0, CHUNKS)
    def _(chunk):
        state_copy(0, chunk).wait_send()

    for level in range(1, ctx_bits):
        @pl.when(wanted[level] == 1)
        def _():
            @pl.loop(0, counts[level])
            def _(n):
                @pl.when(((n < direct) | (skips == 1)) if level == 2 else n >= 0)
                def _():
                    state_copy(level, ours(n)).wait_send()

        if level == 2:
            @pl.when(skips == 1)
            def _():
                for n in range(direct, half):
                    over_copy(ours(n)).wait_send()

        if level > 1:
            @pl.when(digits[level] == 1)
            def _():
                @pl.loop(0, half)
                def _(n):
                    hand_copy(level, ours(n)).wait_send()

    @pl.loop(0, tiles)
    def _(tile):
        at = pl.ds(pl.multiple_of(tile * TILE, TILE), TILE)
        p_copy(tile).wait_recv()
        out[:, at] = (own[:, at] + p_recv[tile].astype(F32)).astype(BF16)


def on_device(query_rows, key_rows, value_rows, level_gate, out_weight):
    tokens, cols = query_rows.shape
    levels, heads, _ = level_gate.shape
    width = cols // heads
    model = out_weight.shape[1]
    rows = tokens // lax.axis_size("head")
    ctx_size = lax.axis_size("ctx")
    ctx_bits = ctx_size.bit_length() - 1
    tiles = model // TILE
    near = len(buckets_of(tokens // C))
    dma = pltpu.SemaphoreType.DMA
    flops = 2 * tokens * cols * (model + 2 * C + width * 7)
    operands = [
        pltpu.with_memory_space_constraint(x, pltpu.HBM)
        for x in (query_rows, key_rows, value_rows, level_gate, out_weight)
    ]
    return pl.pallas_call(
        functools.partial(kernel, ctx_size, heads, levels),
        out_shape=pltpu.VMEM((rows, model), BF16),
        in_specs=[pl.BlockSpec(memory_space=pl.ANY)] * 5,
        out_specs=pl.BlockSpec(memory_space=pltpu.VMEM),
        scratch_shapes=[
            pltpu.VMEM((tokens, cols), BF16),
            pltpu.VMEM((tokens, cols), BF16),
            pltpu.VMEM((tokens, cols), BF16),
            pltpu.VMEM((levels, heads, tokens), F32),
            pltpu.VMEM((heads, tokens, -(-levels // 8) * 8), F32),
            pltpu.VMEM((2, cols, model), BF16),
            pltpu.VMEM((tokens, cols), F32),
            pltpu.VMEM((heads, width, width), F32),
            pltpu.VMEM((heads, near, width, width), BF16),
            pltpu.VMEM((ctx_bits, heads, width, width), BF16),
            pltpu.VMEM((heads, ctx_bits * width, width), BF16),
            pltpu.VMEM((heads, 2 * C, ctx_bits * width), BF16),
            pltpu.VMEM((2, rows, cols), BF16),
            pltpu.VMEM((2, rows, cols), BF16),
            pltpu.VMEM((2, rows, cols), BF16),
            pltpu.VMEM((tiles, rows, TILE), BF16),
            pltpu.VMEM((tiles, rows, TILE), BF16),
            pltpu.VMEM((rows, model), F32),
            dma((7,)),
            dma((ctx_bits, CHUNKS)),
            dma((ctx_bits, CHUNKS)),
            dma((ctx_bits, CHUNKS)),
            dma((CHUNKS,)),
            dma((tiles,)),
            dma((tiles,)),
            dma((2, GROUPS)),
            dma((2, GROUPS)),
            dma((tiles,)),
            dma((tiles,)),
        ],
        compiler_params=pltpu.CompilerParams(
            collective_id=0, has_side_effects=True, vmem_limit_bytes=54 * 1024 * 1024
        ),
        cost_estimate=pl.CostEstimate(
            flops=flops, bytes_accessed=20 * 1024 * 1024, transcendentals=tokens * heads
        ),
        name="levels_project",
    )(*operands)


def solution(mesh):
    in_specs = (
        P("ctx", "head"),
        P("ctx", "head"),
        P("ctx", "head"),
        P(None, "head", "ctx"),
        P("head", None),
    )
    out_specs = P(("ctx", "head"), None)
    return jax.shard_map(
        on_device, mesh=mesh, in_specs=in_specs, out_specs=out_specs, check_vma=False
    )
```
